512 devices in a mesh: lev: 8 (over z_lo, core), tile: 64 (over z_hi, y, x).
Axes of the slice: x: 4, y: 8, z: 8 (z_hi: 2, z_lo: 4; z = z_hi * 4 + z_lo), core: 2. Of those that a mesh axis runs over, the one named last changes fastest.
Arguments:
- adjoint: float32 [5, 64, 1024, 256], P(None, 'lev', 'tile'), may hold values from -6 to 6
- courant: float32 [2, 64, 1024, 256], P(None, 'lev', 'tile'), may hold values from -0.6 to 0.6
- metric: float32 [2, 64, 1024, 256], P(None, 'lev', 'tile'), may hold values from 0.5 to 2
- pivot_inverse: float32 [4, 64, 1024, 256], P(None, 'lev', 'tile'), may hold values from -0.06 to 0.2
- lower_gain: float32 [4, 64, 1024, 256], P(None, 'lev', 'tile'), may hold values from -0.5 to 1
- upper_gain: float32 [4, 64, 1024, 256], P(None, 'lev', 'tile'), may hold values from -0.5 to 1
Outputs:
- stepped: float32 [5, 64, 1024, 256], P(None, 'lev', 'tile')
The draws below stay inside these ranges and needn't reach their ends.
All inputs are finite; a program needn't handle non-finite values.
Results may differ from the reference program's by a relative error of at most 0.00002.
Values sent between devices are 32-bit elements; how exact they have to be, the bound alone decides.
A program may use at most 64 MiB of HBM per device.

```python
import math
import jax
import jax.numpy as jnp
from jax import lax

CY = 256
LEVELS = 64
NX = 1024


def draw_pivot_inverse(key, part):
    domain_extent = (2, LEVELS, NX, CY)
    first_key, second_random_key = jax.random.split(key)
    main_diagonal = jnp.exp(jax.random.uniform(first_key, domain_extent, jnp.float32, math.log(0.05), math.log(0.2)))
    crossing = jax.random.uniform(second_random_key, domain_extent, jnp.float32, -0.06, 0.06)
    return jnp.stack([main_diagonal[0], crossing[0], crossing[1], main_diagonal[1]])


def gain_draw(key, marker):
    seeded = jax.random.fold_in(key, marker)
    first_key, second_random_key, third_key = jax.random.split(seeded, 3)
    domain_extent = (2, LEVELS, NX, CY)
    rate = jnp.exp(jax.random.uniform(first_key, domain_extent, jnp.float32, min(math.log(0.3 / LEVELS), math.log(1.0 / 40.0)), math.log(1.0 / 30.0)))
    main_diagonal = jnp.exp(-rate)
    pulse_groups = jax.random.bernoulli(second_random_key, 1.0 / 32.0, domain_extent)
    main_diagonal = jnp.where(pulse_groups, 0.6 * main_diagonal, main_diagonal)
    crossing = jax.random.uniform(third_key, domain_extent, jnp.float32, -1.0, 1.0) * 0.5 * (1.0 - main_diagonal)
    return jnp.stack([main_diagonal[0], crossing[0], crossing[1], main_diagonal[1]])


def draw_lower_gain(key, part):
    return gain_draw(key, 11)


def draw_upper_gain(key, part):
    return gain_draw(key, 23)


def block_scale(key, shape, shards, low, largest):
    def one(position, blocks):
        steps = jax.random.uniform(jax.random.fold_in(jax.random.fold_in(key, 6), position), (blocks,), jnp.float32, low / len(shards), largest / len(shards))
        return jnp.repeat(jnp.exp(steps), shape[position] // blocks).reshape((-1,) + (1,) * (len(shape) - position - 1))

    gain = one(*shards[0])
    for cut in shards[1:]:
        gain = gain * one(*cut)
    return gain


def centred(rng, dims, scale, limit, shards=(), kind=jnp.bfloat16):
    result = scale * jax.random.normal(rng, dims, jnp.float32)
    if shards:
        result = result * block_scale(rng, dims, shards, -0.22, 0.18)
    return jnp.clip(result, -limit, limit).astype(kind)


def setup_inputs(seed: int = 0) -> dict:
    key_of = jax.random.split(jax.random.key(seed), 7)
    adjoint = centred(key_of[0], (5, LEVELS, NX, CY), 1.0, 6.0, ((1, 8), (2, 64)), jnp.float32)
    courant = jnp.clip(jax.random.uniform(key_of[1], (2, LEVELS, NX, CY), jnp.float32, -0.6, 0.6) * block_scale(key_of[1], (2, LEVELS, NX, CY), ((1, 8), (2, 64)), -0.4, 0.0), -0.6, 0.6)
    metric = jnp.clip(jnp.exp(math.log(2.0) - 1.3862944 * jax.random.uniform(key_of[2], (2, LEVELS, NX, CY), jnp.float32) ** block_scale(key_of[2], (2, LEVELS, NX, CY), ((1, 8), (2, 64)), -0.2, 0.2)), 0.5, 2.0)
    pivot_inverse = draw_pivot_inverse(jax.random.fold_in(key_of[6], 71), 0)
    lower_gain = draw_lower_gain(jax.random.fold_in(key_of[6], 71), 0)
    upper_gain = draw_upper_gain(jax.random.fold_in(key_of[6], 71), 0)
    return {"adjoint": adjoint, "courant": courant, "metric": metric, "pivot_inverse": pivot_inverse, "lower_gain": lower_gain, "upper_gain": upper_gain}


def centered_roll(values, axis_id):
    ahead_one = jnp.roll(values, -1, axis_id)
    behind_one = jnp.roll(values, 1, axis_id)
    ahead_two = jnp.roll(values, -2, axis_id)
    behind_two = jnp.roll(values, 2, axis_id)
    return (8.0 * (ahead_one - behind_one) - (ahead_two - behind_two)) / 12.0


def mat_vec(system_matrix, vector):
    return jnp.stack([system_matrix[0] * vector[0] + system_matrix[1] * vector[1],
                      system_matrix[2] * vector[0] + system_matrix[3] * vector[1]])


def chain_run(coupling, forcing, initial, backward):
    def advance(state, inputs):
        fresh = mat_vec(inputs[0], state) + inputs[1]
        return fresh, fresh

    final_state, states = lax.scan(advance, initial,
                                   (jnp.moveaxis(coupling, 1, 0), jnp.moveaxis(forcing, 1, 0)),
                                   reverse=backward)
    return jnp.moveaxis(states, 0, 1)


def reference(adjoint, courant, metric, pivot_inverse, lower_gain, upper_gain):
    advected = adjoint + centered_roll(courant[0] * adjoint, 2) + centered_roll(courant[1] * adjoint, 3)
    pressure_field = advected[4] + centered_roll(metric[0] * adjoint[0], 1) + centered_roll(metric[1] * adjoint[1], 2)
    forcing = mat_vec(pivot_inverse, jnp.stack([advected[2], pressure_field]))
    initial = jnp.zeros((2,) + adjoint.shape[2:], jnp.float32)
    lowered = chain_run(lower_gain, forcing, initial, False)
    solved = chain_run(upper_gain, lowered, initial, True)
    return jnp.stack([advected[0], advected[1], solved[0], advected[3], solved[1]])
```

```python
import functools

import jax
import jax.numpy as jnp
from jax import lax
from jax.experimental import pallas as pl
from jax.experimental.pallas import tpu as pltpu
from jax.sharding import PartitionSpec as P

MESH = pl.DeviceIdType.MESH
NEAR = 8.0 / 12.0
FAR = 1.0 / 12.0
TILE_ROWS = 8
TILE_LANES = 128
HALF = TILE_ROWS // 2


def difference(ahead_one, behind_one, ahead_two, behind_two):
    return NEAR * (ahead_one - behind_one) - FAR * (ahead_two - behind_two)


def rows_inside(values):
    count = values.shape[0]
    row = lax.broadcasted_iota(jnp.int32, values.shape, 0)
    return difference(
        jnp.where(row < count - 1, pltpu.roll(values, count - 1, 0), 0.0),
        jnp.where(row >= 1, pltpu.roll(values, 1, 0), 0.0),
        jnp.where(row < count - 2, pltpu.roll(values, count - 2, 0), 0.0),
        jnp.where(row >= 2, pltpu.roll(values, 2, 0), 0.0),
    )


def lanes_around(values):
    count = values.shape[1]
    return difference(
        pltpu.roll(values, count - 1, 1),
        pltpu.roll(values, 1, 1),
        pltpu.roll(values, count - 2, 1),
        pltpu.roll(values, 2, 1),
    )


def low_edge(row, two_below, one_below):
    return jnp.where(
        row == 0, FAR * two_below - NEAR * one_below, jnp.where(row == 1, FAR * one_below, 0.0)
    )


def high_edge(row, one_above, two_above):
    return jnp.where(
        row == TILE_ROWS - 1,
        NEAR * one_above - FAR * two_above,
        jnp.where(row == TILE_ROWS - 2, -FAR * one_above, 0.0),
    )


def times(left, right):
    return (
        left[0] * right[0] + left[1] * right[2],
        left[0] * right[1] + left[1] * right[3],
        left[2] * right[0] + left[3] * right[2],
        left[2] * right[1] + left[3] * right[3],
    )


def apply(matrix, vector):
    return (
        matrix[0] * vector[0] + matrix[1] * vector[1],
        matrix[2] * vector[0] + matrix[3] * vector[1],
    )


def plus(left, right):
    return tuple(a + b for a, b in zip(left, right))


def swapped(values):
    return pltpu.roll(values, HALF, 0)


def pack(upper, first, second):
    return (
        jnp.where(upper, first, swapped(second)),
        jnp.where(upper, swapped(first), second),
    )


def unpack(upper, low, high):
    return (
        jnp.where(upper, low, swapped(high)),
        jnp.where(upper, swapped(low), high),
    )


def kernel(
    levs,
    tiles,
    adjoint_hbm,
    courant_hbm,
    metric_hbm,
    pivot_hbm,
    lower_hbm,
    upper_hbm,
    out_hbm,
    adjoint,
    courant,
    metric,
    pivot,
    lower,
    upper,
    stepped,
    forcing,
    edge_send,
    edge_recv,
    side_send,
    side_recv,
    block_send,
    block_recv,
    carry_send,
    carry_recv,
    state_send,
    state_recv,
    load_sem,
    store_sem,
    edge_sems,
    side_sems,
    block_sems,
    carry_sems,
    state_sems,
):
    lev = lax.axis_index("lev")
    tile = lax.axis_index("tile")
    levels, rows, lanes = adjoint.shape[1:]
    right = lax.rem(tile + 1, tiles)
    left = lax.rem(tile + tiles - 1, tiles)

    def peer(offset):
        return lax.rem(lev + offset, levs)

    def slot_of(source):
        return lax.rem(lev + levs - source, levs)

    barrier = pltpu.get_barrier_semaphore()
    for target in (left, right):
        pl.semaphore_signal(barrier, inc=1, device_id=(lev, target), device_id_type=MESH)
    for offset in range(1, levs):
        pl.semaphore_signal(barrier, inc=1, device_id=(peer(offset), tile), device_id_type=MESH)

    loads = [
        pltpu.make_async_copy(source, target, load_sem.at[i])
        for i, (source, target) in enumerate(
            (
                (adjoint_hbm, adjoint),
                (courant_hbm, courant),
                (metric_hbm, metric),
                (lower_hbm, lower),
                (upper_hbm, upper),
                (pivot_hbm, pivot),
            )
        )
    ]
    for load in loads:
        load.start()
    for load in loads[:3]:
        load.wait()

    def critical(level, carry):
        drift = courant[0, level]
        side = courant[1, level]
        for place, field in ((0, 2), (1, 4)):
            here = adjoint[field, level]
            along = drift * here
            across = side * here
            if place:
                along = along + metric[0, level] * adjoint[0, level]
                across = across + metric[1, level] * adjoint[1, level]
            edge_send[0, place, level] = along[:2]
            edge_send[1, place, level] = along[rows - 2 :]
            stepped[field, level] = here + rows_inside(along) + lanes_around(across)
        return carry

    lax.fori_loop(0, levels, critical, 0)

    for load in loads[3:5]:
        load.wait()

    tile_shape = (TILE_ROWS, TILE_LANES)
    row = lax.broadcasted_iota(jnp.int32, tile_shape, 0)
    is_upper = row < HALF
    halves = lanes // TILE_LANES

    def part(index):
        return pl.ds(pl.multiple_of(index * TILE_LANES, TILE_LANES), TILE_LANES)

    def summarise(index, carry):
        for band in range(rows // TILE_ROWS):
            where = (pl.ds(band * TILE_ROWS, TILE_ROWS), part(index))

            def gain(ref, level):
                return tuple(ref[entry, level, where[0], where[1]] for entry in range(4))

            down = [gain(lower, 0)]
            for level in range(1, levels):
                down.append(times(gain(lower, level), down[-1]))
            up = gain(upper, levels - 1)
            mixed = down[-1]
            for level in range(levels - 2, -1, -1):
                step = gain(upper, level)
                mixed = plus(times(step, mixed), down[level])
                up = times(step, up)
            target = 2 * (band * halves + index)
            for place, matrix in enumerate((down[-1], up, mixed)):
                for kind, pair in enumerate(((matrix[0], matrix[3]), (matrix[1], matrix[2]))):
                    low, high = pack(is_upper, *pair)
                    block_send[target, 2 * place + kind] = low
                    block_send[target + 1, 2 * place + kind] = high
        return carry

    lax.fori_loop(0, halves, summarise, 0)

    pl.semaphore_wait(barrier, levs + 1)

    def to_sides(source, target, sems):
        copies = []
        for direction, where in ((0, left), (1, right)):
            copies.append(
                pltpu.make_async_remote_copy(
                    src_ref=source.at[direction],
                    dst_ref=target.at[direction],
                    send_sem=sems.at[0, direction],
                    recv_sem=sems.at[1, direction],
                    device_id=(lev, where),
                    device_id_type=MESH,
                )
            )
        for copy in copies:
            copy.start()
        return copies

    def to_levels(source, target, sems):
        copies = []
        for offset in range(1, levs):
            copies.append(
                pltpu.make_async_remote_copy(
                    src_ref=source.at[peer(offset)],
                    dst_ref=target.at[offset],
                    send_sem=sems.at[0, offset],
                    recv_sem=sems.at[1, offset],
                    device_id=(peer(offset), tile),
                    device_id_type=MESH,
                )
            )
        for copy in copies:
            copy.start()
        target[0] = source[lev]
        return copies

    edge_copies = to_sides(edge_send, edge_recv, edge_sems)
    block_copies = to_levels(block_send, block_recv, block_sems)

    def passive(level, carry):
        drift = courant[0, level]
        side = courant[1, level]
        for place, field in enumerate((0, 1, 3)):
            here = adjoint[field, level]
            along = drift * here
            side_send[0, place, level] = along[:2]
            side_send[1, place, level] = along[rows - 2 :]
            stepped[field, level] = here + rows_inside(along) + lanes_around(side * here)
        return carry

    lax.fori_loop(0, levels, passive, 0)
    side_copies = to_sides(side_send, side_recv, side_sems)

    loads[5].wait()
    for copy in edge_copies:
        copy.wait_recv()

    def correction(ref, place, level, band, lane_part):
        total = None
        if band == 0:
            total = low_edge(
                row,
                ref[1, place, level, pl.ds(0, 1), lane_part],
                ref[1, place, level, pl.ds(1, 1), lane_part],
            )
        if band == rows // TILE_ROWS - 1:
            high = high_edge(
                row,
                ref[0, place, level, pl.ds(0, 1), lane_part],
                ref[0, place, level, pl.ds(1, 1), lane_part],
            )
            total = high if total is None else total + high
        return total

    def force(index, carry):
        lane_part = part(index)
        for band in range(rows // TILE_ROWS):
            row_part = pl.ds(band * TILE_ROWS, TILE_ROWS)

            def gain(ref, level):
                return tuple(ref[entry, level, row_part, lane_part] for entry in range(4))

            falling = []
            for level in range(levels):
                pair = []
                for place, field in ((0, 2), (1, 4)):
                    value = stepped[field, level, row_part, lane_part]
                    fix = correction(edge_recv, place, level, band, lane_part)
                    pair.append(value if fix is None else value + fix)
                fresh = apply(gain(pivot, level), pair)
                for place in range(2):
                    forcing[place, level, row_part, lane_part] = fresh[place]
                if falling:
                    fresh = plus(apply(gain(lower, level), falling[-1]), fresh)
                falling.append(fresh)
            rising = falling[-1]
            for level in range(levels - 2, -1, -1):
                rising = plus(apply(gain(upper, level), rising), falling[level])
            target = 2 * (band * halves + index)
            for place, pair in enumerate((falling[-1], rising)):
                low, high = pack(is_upper, *pair)
                carry_send[target, place] = low
                carry_send[target + 1, place] = high
        return carry

    lax.fori_loop(0, halves, force, 0)
    carry_copies = to_levels(carry_send, carry_recv, carry_sems)

    for copy in block_copies:
        copy.wait_recv()
    for copy in carry_copies:
        copy.wait_recv()

    state = jnp.zeros(tile_shape, jnp.float32)
    states = []
    for block in range(levs):
        states.append(state)
        state_send[block, 0] = state
        if block < levs - 1:
            slot = slot_of(block)
            state = (
                block_recv[slot, 0] * state
                + block_recv[slot, 1] * swapped(state)
                + carry_recv[slot, 0]
            )
    state = jnp.zeros(tile_shape, jnp.float32)
    for block in range(levs - 1, -1, -1):
        state_send[block, 1] = state
        if block:
            slot = slot_of(block)
            state = (
                block_recv[slot, 2] * state
                + block_recv[slot, 3] * swapped(state)
                + block_recv[slot, 4] * states[block]
                + block_recv[slot, 5] * swapped(states[block])
                + carry_recv[slot, 1]
            )
    state_copies = to_levels(state_send, state_recv, state_sems)

    for copy in side_copies:
        copy.wait_recv()

    def finish(level, carry):
        lane_all = pl.ds(0, lanes)
        wide = lax.broadcasted_iota(jnp.int32, (TILE_ROWS, lanes), 0)
        for place, field in enumerate((0, 1, 3)):
            top = pl.ds(0, TILE_ROWS)
            bottom = pl.ds(rows - TILE_ROWS, TILE_ROWS)
            stepped[field, level, top] += low_edge(
                wide,
                side_recv[1, place, level, pl.ds(0, 1)],
                side_recv[1, place, level, pl.ds(1, 1)],
            )
            stepped[field, level, bottom] += high_edge(
                wide,
                side_recv[0, place, level, pl.ds(0, 1)],
                side_recv[0, place, level, pl.ds(1, 1)],
            )
        return carry

    lax.fori_loop(0, levels, finish, 0)

    stores = {
        field: pltpu.make_async_copy(stepped.at[field], out_hbm.at[field], store_sem.at[field])
        for field in range(5)
    }
    for field in (0, 1, 3):
        stores[field].start()

    for copy in state_copies:
        copy.wait_recv()

    def settle(index, carry):
        lane_part = part(index)
        for band in range(rows // TILE_ROWS):
            row_part = pl.ds(band * TILE_ROWS, TILE_ROWS)

            def gain(ref, level):
                return tuple(ref[entry, level, row_part, lane_part] for entry in range(4))

            source = 2 * (band * halves + index)
            low, high = slot_of(source), slot_of(source + 1)
            state = unpack(is_upper, state_recv[low, 0], state_recv[high, 0])
            falling = []
            for level in range(levels):
                fresh = tuple(forcing[place, level, row_part, lane_part] for place in range(2))
                state = plus(apply(gain(lower, level), state), fresh)
                falling.append(state)
            state = unpack(is_upper, state_recv[low, 1], state_recv[high, 1])
            for level in range(levels - 1, -1, -1):
                state = plus(apply(gain(upper, level), state), falling[level])
                stepped[2, level, row_part, lane_part] = state[0]
                stepped[4, level, row_part, lane_part] = state[1]
        return carry

    lax.fori_loop(0, halves, settle, 0)
    for field in (2, 4):
        stores[field].start()
    for copy in edge_copies + side_copies + block_copies + carry_copies + state_copies:
        copy.wait_send()
    for field in range(5):
        stores[field].wait()


def local(levs, tiles, adjoint, courant, metric, pivot_inverse, lower_gain, upper_gain):
    fields, levels, rows, lanes = adjoint.shape
    arrays = (adjoint, courant, metric, pivot_inverse, lower_gain, upper_gain)
    small = (TILE_ROWS, TILE_LANES)

    def vmem(*shape):
        return pltpu.VMEM(shape, jnp.float32)

    return pl.pallas_call(
        functools.partial(kernel, levs, tiles),
        out_shape=jax.ShapeDtypeStruct(adjoint.shape, jnp.float32),
        in_specs=[pl.BlockSpec(memory_space=pl.ANY)] * len(arrays),
        out_specs=pl.BlockSpec(memory_space=pl.ANY),
        scratch_shapes=[vmem(*array.shape) for array in arrays]
        + [
            vmem(*adjoint.shape),
            vmem(2, levels, rows, lanes),
            vmem(2, 2, levels, 2, lanes),
            vmem(2, 2, levels, 2, lanes),
            vmem(2, 3, levels, 2, lanes),
            vmem(2, 3, levels, 2, lanes),
            vmem(levs, 6, *small),
            vmem(levs, 6, *small),
            vmem(levs, 2, *small),
            vmem(levs, 2, *small),
            vmem(levs, 2, *small),
            vmem(levs, 2, *small),
            pltpu.SemaphoreType.DMA((len(arrays),)),
            pltpu.SemaphoreType.DMA((fields,)),
            pltpu.SemaphoreType.DMA((2, 2)),
            pltpu.SemaphoreType.DMA((2, 2)),
            pltpu.SemaphoreType.DMA((2, levs)),
            pltpu.SemaphoreType.DMA((2, levs)),
            pltpu.SemaphoreType.DMA((2, levs)),
        ],
        compiler_params=pltpu.CompilerParams(collective_id=0, has_side_effects=True),
    )(*arrays)


def solution(mesh):
    placed = P(None, "lev", "tile", None)
    return jax.shard_map(
        functools.partial(local, mesh.shape["lev"], mesh.shape["tile"]),
        mesh=mesh,
        in_specs=(placed,) * 6,
        out_specs=placed,
        check_vma=False,
    )
```

```python
import functools

import jax
import jax.numpy as jnp
from jax import lax
from jax.experimental import pallas as pl
from jax.experimental.pallas import tpu as pltpu
from jax.sharding import PartitionSpec as P

MESH = pl.DeviceIdType.MESH
NEAR = 8.0 / 12.0
FAR = 1.0 / 12.0
TILE_ROWS = 8
TILE_LANES = 128


def difference(ahead_one, behind_one, ahead_two, behind_two):
    return NEAR * (ahead_one - behind_one) - FAR * (ahead_two - behind_two)


def rows_inside(values):
    count = values.shape[0]
    row = lax.broadcasted_iota(jnp.int32, values.shape, 0)
    return difference(
        jnp.where(row < count - 1, pltpu.roll(values, count - 1, 0), 0.0),
        jnp.where(row >= 1, pltpu.roll(values, 1, 0), 0.0),
        jnp.where(row < count - 2, pltpu.roll(values, count - 2, 0), 0.0),
        jnp.where(row >= 2, pltpu.roll(values, 2, 0), 0.0),
    )


def lanes_around(values):
    count = values.shape[1]
    return difference(
        pltpu.roll(values, count - 1, 1),
        pltpu.roll(values, 1, 1),
        pltpu.roll(values, count - 2, 1),
        pltpu.roll(values, 2, 1),
    )


def low_edge(row, two_below, one_below):
    return jnp.where(
        row == 0, FAR * two_below - NEAR * one_below, jnp.where(row == 1, FAR * one_below, 0.0)
    )


def high_edge(row, one_above, two_above):
    return jnp.where(
        row == TILE_ROWS - 1,
        NEAR * one_above - FAR * two_above,
        jnp.where(row == TILE_ROWS - 2, -FAR * one_above, 0.0),
    )


def times(left, right):
    return (
        left[0] * right[0] + left[1] * right[2],
        left[0] * right[1] + left[1] * right[3],
        left[2] * right[0] + left[3] * right[2],
        left[2] * right[1] + left[3] * right[3],
    )


def apply(matrix, vector):
    return (
        matrix[0] * vector[0] + matrix[1] * vector[1],
        matrix[2] * vector[0] + matrix[3] * vector[1],
    )


def plus(left, right):
    return tuple(a + b for a, b in zip(left, right))


def kernel(
    levs,
    tiles,
    adjoint_hbm,
    courant_hbm,
    metric_hbm,
    pivot_hbm,
    lower_hbm,
    upper_hbm,
    stepped,
    adjoint,
    courant,
    metric,
    pivot,
    lower,
    upper,
    forcing,
    edge_send,
    edge_recv,
    side_send,
    side_recv,
    block_send,
    block_recv,
    carry_send,
    carry_recv,
    state_send,
    state_recv,
    load_sem,
    edge_sems,
    side_sems,
    block_sems,
    carry_sems,
    state_sems,
):
    lev = lax.axis_index("lev")
    tile = lax.axis_index("tile")
    levels, rows, lanes = adjoint.shape[1:]
    right = lax.rem(tile + 1, tiles)
    left = lax.rem(tile + tiles - 1, tiles)

    def peer(offset):
        return lax.rem(lev + offset, levs)

    def slot_of(source):
        return lax.rem(lev + levs - source, levs)

    parts = block_send.shape[0]
    first = (levs - parts) // 2

    def solves(device):
        return jnp.logical_and(device >= first, device < first + parts)

    solver = solves(lev)

    barrier = pltpu.get_barrier_semaphore()
    for target in (left, right):
        pl.semaphore_signal(barrier, inc=1, device_id=(lev, target), device_id_type=MESH)
    for offset in range(1, levs):

        @pl.when(jnp.logical_or(solver, solves(peer(offset))))
        def _():
            pl.semaphore_signal(barrier, inc=1, device_id=(peer(offset), tile), device_id_type=MESH)

    order = (
        [(adjoint_hbm.at[field], adjoint.at[field]) for field in (0, 2, 4)]
        + [(courant_hbm.at[0], courant.at[0]), (metric_hbm.at[0], metric.at[0])]
        + [(lower_hbm, lower), (upper_hbm, upper)]
        + [(courant_hbm.at[1], courant.at[1]), (metric_hbm.at[1], metric.at[1])]
        + [(adjoint_hbm.at[field], adjoint.at[field]) for field in (1, 3)]
        + [(pivot_hbm, pivot)]
    )
    loads = [
        pltpu.make_async_copy(source, target, load_sem.at[i])
        for i, (source, target) in enumerate(order)
    ]
    for load in loads:
        load.start()
    for load in loads[:5]:
        load.wait()

    def weighted(level, field):
        along = courant[0, level] * adjoint[field, level]
        if field == 4:
            along = along + metric[0, level] * adjoint[0, level]
        return along

    def edges(level, carry):
        for place, field in ((0, 2), (1, 4)):
            along = weighted(level, field)
            edge_send[0, place, level] = along[:2]
            edge_send[1, place, level] = along[rows - 2 :]
        return carry

    lax.fori_loop(0, levels, edges, 0)

    @pl.when(solver)
    def _():
        pl.semaphore_wait(barrier, levs + 1)

    @pl.when(jnp.logical_not(solver))
    def _():
        pl.semaphore_wait(barrier, parts + 2)

    def to_sides(source, target, sems):
        copies = []
        for direction, where in ((0, left), (1, right)):
            copies.append(
                pltpu.make_async_remote_copy(
                    src_ref=source.at[direction],
                    dst_ref=target.at[direction],
                    send_sem=sems.at[0, direction],
                    recv_sem=sems.at[1, direction],
                    device_id=(lev, where),
                    device_id_type=MESH,
                )
            )
        for copy in copies:
            copy.start()
        return copies

    def level_copy(source, target, sems, offset, place):
        return pltpu.make_async_remote_copy(
            src_ref=source.at[place],
            dst_ref=target.at[offset],
            send_sem=sems.at[0, offset],
            recv_sem=sems.at[1, offset],
            device_id=(peer(offset), tile),
            device_id_type=MESH,
        )

    def part_of(device):
        return jnp.clip(device - first, 0, parts - 1)

    def to_solvers(source, target, sems, starting):
        for offset in range(1, levs):

            @pl.when(solves(peer(offset)))
            def _():
                copy = level_copy(source, target, sems, offset, part_of(peer(offset)))
                if starting:
                    copy.start()
                else:
                    copy.wait_send()

    def at_solver(source, target, sems):
        target[0] = source[part_of(lev)]
        for offset in range(1, levs):
            level_copy(source, target, sems, offset, 0).wait_recv()

    edge_copies = to_sides(edge_send, edge_recv, edge_sems)

    for load in loads[5:7]:
        load.wait()

    tile_shape = (TILE_ROWS, TILE_LANES)
    row = lax.broadcasted_iota(jnp.int32, tile_shape, 0)
    halves = lanes // TILE_LANES

    def part(index):
        return pl.ds(pl.multiple_of(index * TILE_LANES, TILE_LANES), TILE_LANES)

    def summarise(index, carry):
        for band in range(rows // TILE_ROWS):
            where = (pl.ds(band * TILE_ROWS, TILE_ROWS), part(index))

            def gain(ref, level):
                return tuple(ref[entry, level, where[0], where[1]] for entry in range(4))

            down = [gain(lower, 0)]
            for level in range(1, levels):
                down.append(times(gain(lower, level), down[-1]))
            up = gain(upper, levels - 1)
            mixed = down[-1]
            for level in range(levels - 2, -1, -1):
                step = gain(upper, level)
                mixed = plus(times(step, mixed), down[level])
                up = times(step, up)
            target = band * halves + index
            for place, matrix in enumerate((down[-1], up, mixed)):
                for entry in range(4):
                    block_send[target, 4 * place + entry] = matrix[entry]
        return carry

    lax.fori_loop(0, halves, summarise, 0)

    to_solvers(block_send, block_recv, block_sems, True)

    for load in loads[7:]:
        load.wait()

    def critical(level, carry):
        for field in (2, 4):
            here = adjoint[field, level]
            across = courant[1, level] * here
            if field == 4:
                across = across + metric[1, level] * adjoint[1, level]
            along = rows_inside(weighted(level, field))
            stepped[field, level] = here + along + lanes_around(across)
        return carry

    lax.fori_loop(0, levels, critical, 0)

    def passive(level, carry):
        drift = courant[0, level]
        side = courant[1, level]
        for place, field in enumerate((0, 1, 3)):
            here = adjoint[field, level]
            along = drift * here
            side_send[0, place, level] = along[:2]
            side_send[1, place, level] = along[rows - 2 :]
            stepped[field, level] = here + rows_inside(along) + lanes_around(side * here)
        return carry

    lax.fori_loop(0, levels, passive, 0)
    side_copies = to_sides(side_send, side_recv, side_sems)

    for copy in edge_copies:
        copy.wait_recv()

    def correction(ref, place, level, band, lane_part):
        total = None
        if band == 0:
            total = low_edge(
                row,
                ref[1, place, level, pl.ds(0, 1), lane_part],
                ref[1, place, level, pl.ds(1, 1), lane_part],
            )
        if band == rows // TILE_ROWS - 1:
            high = high_edge(
                row,
                ref[0, place, level, pl.ds(0, 1), lane_part],
                ref[0, place, level, pl.ds(1, 1), lane_part],
            )
            total = high if total is None else total + high
        return total

    def force(index, carry):
        lane_part = part(index)
        for band in range(rows // TILE_ROWS):
            row_part = pl.ds(band * TILE_ROWS, TILE_ROWS)

            def gain(ref, level):
                return tuple(ref[entry, level, row_part, lane_part] for entry in range(4))

            falling = []
            for level in range(levels):
                pair = []
                for place, field in ((0, 2), (1, 4)):
                    value = stepped[field, level, row_part, lane_part]
                    fix = correction(edge_recv, place, level, band, lane_part)
                    pair.append(value if fix is None else value + fix)
                fresh = apply(gain(pivot, level), pair)
                for place in range(2):
                    forcing[place, level, row_part, lane_part] = fresh[place]
                if falling:
                    fresh = plus(apply(gain(lower, level), falling[-1]), fresh)
                falling.append(fresh)
            rising = falling[-1]
            for level in range(levels - 2, -1, -1):
                rising = plus(apply(gain(upper, level), rising), falling[level])
            target = band * halves + index
            for place, value in enumerate(falling[-1] + rising):
                carry_send[target, place] = value
        return carry

    lax.fori_loop(0, halves, force, 0)
    to_solvers(carry_send, carry_recv, carry_sems, True)

    @pl.when(solver)
    def _():
        at_solver(block_send, block_recv, block_sems)
        at_solver(carry_send, carry_recv, carry_sems)

        def matrix(slot, place):
            return tuple(block_recv[slot, 4 * place + entry] for entry in range(4))

        def vector(slot, place):
            return tuple(carry_recv[slot, 2 * place + entry] for entry in range(2))

        nothing = jnp.zeros(tile_shape, jnp.float32)
        state = (nothing, nothing)
        states = []
        for block in range(levs):
            states.append(state)
            for entry in range(2):
                state_send[block, entry] = state[entry]
            if block < levs - 1:
                slot = slot_of(block)
                state = plus(apply(matrix(slot, 0), state), vector(slot, 0))
        state = (nothing, nothing)
        for block in range(levs - 1, -1, -1):
            for entry in range(2):
                state_send[block, 2 + entry] = state[entry]
            if block:
                slot = slot_of(block)
                state = plus(
                    apply(matrix(slot, 1), state),
                    plus(apply(matrix(slot, 2), states[block]), vector(slot, 1)),
                )
        for offset in range(1, levs):
            level_copy(state_send, state_recv, state_sems, offset, peer(offset)).start()
        state_recv[0] = state_send[lev]

    for copy in side_copies:
        copy.wait_recv()

    def finish(level, carry):
        wide = lax.broadcasted_iota(jnp.int32, (TILE_ROWS, lanes), 0)
        for place, field in enumerate((0, 1, 3)):
            top = pl.ds(0, TILE_ROWS)
            bottom = pl.ds(rows - TILE_ROWS, TILE_ROWS)
            stepped[field, level, top] += low_edge(
                wide,
                side_recv[1, place, level, pl.ds(0, 1)],
                side_recv[1, place, level, pl.ds(1, 1)],
            )
            stepped[field, level, bottom] += high_edge(
                wide,
                side_recv[0, place, level, pl.ds(0, 1)],
                side_recv[0, place, level, pl.ds(1, 1)],
            )
        return carry

    lax.fori_loop(0, levels, finish, 0)

    for offset in range(1, levs):

        @pl.when(solves(lax.rem(lev + levs - offset, levs)))
        def _():
            level_copy(state_send, state_recv, state_sems, offset, 0).wait_recv()

    def settle(index, carry):
        lane_part = part(index)
        for band in range(rows // TILE_ROWS):
            row_part = pl.ds(band * TILE_ROWS, TILE_ROWS)

            def gain(ref, level):
                return tuple(ref[entry, level, row_part, lane_part] for entry in range(4))

            slot = slot_of(first + band * halves + index)
            state = (state_recv[slot, 0], state_recv[slot, 1])
            falling = []
            for level in range(levels):
                fresh = tuple(forcing[place, level, row_part, lane_part] for place in range(2))
                state = plus(apply(gain(lower, level), state), fresh)
                falling.append(state)
            state = (state_recv[slot, 2], state_recv[slot, 3])
            for level in range(levels - 1, -1, -1):
                state = plus(apply(gain(upper, level), state), falling[level])
                stepped[2, level, row_part, lane_part] = state[0]
                stepped[4, level, row_part, lane_part] = state[1]
        return carry

    lax.fori_loop(0, halves, settle, 0)
    for copy in edge_copies + side_copies:
        copy.wait_send()
    to_solvers(block_send, block_recv, block_sems, False)
    to_solvers(carry_send, carry_recv, carry_sems, False)

    @pl.when(solver)
    def _():
        for offset in range(1, levs):
            level_copy(state_send, state_recv, state_sems, offset, 0).wait_send()


def local(levs, tiles, adjoint, courant, metric, pivot_inverse, lower_gain, upper_gain):
    fields, levels, rows, lanes = adjoint.shape
    arrays = (adjoint, courant, metric, pivot_inverse, lower_gain, upper_gain)
    small = (TILE_ROWS, TILE_LANES)
    parts = rows * lanes // (TILE_ROWS * TILE_LANES)

    def vmem(*shape):
        return pltpu.VMEM(shape, jnp.float32)

    return pl.pallas_call(
        functools.partial(kernel, levs, tiles),
        out_shape=pltpu.VMEM(adjoint.shape, jnp.float32),
        in_specs=[pl.BlockSpec(memory_space=pl.ANY)] * len(arrays),
        out_specs=pl.BlockSpec(memory_space=pltpu.VMEM),
        scratch_shapes=[vmem(*array.shape) for array in arrays]
        + [
            vmem(2, levels, rows, lanes),
            vmem(2, 2, levels, 2, lanes),
            vmem(2, 2, levels, 2, lanes),
            vmem(2, 3, levels, 2, lanes),
            vmem(2, 3, levels, 2, lanes),
            vmem(parts, 12, *small),
            vmem(levs, 12, *small),
            vmem(parts, 4, *small),
            vmem(levs, 4, *small),
            vmem(levs, 4, *small),
            vmem(levs, 4, *small),
            pltpu.SemaphoreType.DMA((12,)),
            pltpu.SemaphoreType.DMA((2, 2)),
            pltpu.SemaphoreType.DMA((2, 2)),
            pltpu.SemaphoreType.DMA((2, levs)),
            pltpu.SemaphoreType.DMA((2, levs)),
            pltpu.SemaphoreType.DMA((2, levs)),
        ],
        compiler_params=pltpu.CompilerParams(collective_id=0, has_side_effects=True),
    )(*arrays)


def solution(mesh):
    placed = P(None, "lev", "tile", None)
    return jax.shard_map(
        functools.partial(local, mesh.shape["lev"], mesh.shape["tile"]),
        mesh=mesh,
        in_specs=(placed,) * 6,
        out_specs=placed,
        check_vma=False,
    )
```

```python
import functools

import jax
import jax.numpy as jnp
from jax import lax
from jax.experimental import pallas as pl
from jax.experimental.pallas import tpu as pltpu
from jax.sharding import PartitionSpec as P

MESH = pl.DeviceIdType.MESH
NEAR = 8.0 / 12.0
FAR = 1.0 / 12.0
TILE_ROWS = 8
TILE_LANES = 128


def difference(ahead_one, behind_one, ahead_two, behind_two):
    return NEAR * (ahead_one - behind_one) - FAR * (ahead_two - behind_two)


def rows_inside(values):
    count = values.shape[0]
    row = lax.broadcasted_iota(jnp.int32, values.shape, 0)
    return difference(
        jnp.where(row < count - 1, pltpu.roll(values, count - 1, 0), 0.0),
        jnp.where(row >= 1, pltpu.roll(values, 1, 0), 0.0),
        jnp.where(row < count - 2, pltpu.roll(values, count - 2, 0), 0.0),
        jnp.where(row >= 2, pltpu.roll(values, 2, 0), 0.0),
    )


def lanes_around(values):
    count = values.shape[1]
    return difference(
        pltpu.roll(values, count - 1, 1),
        pltpu.roll(values, 1, 1),
        pltpu.roll(values, count - 2, 1),
        pltpu.roll(values, 2, 1),
    )


def low_edge(row, two_below, one_below):
    return jnp.where(
        row == 0, FAR * two_below - NEAR * one_below, jnp.where(row == 1, FAR * one_below, 0.0)
    )


def high_edge(row, one_above, two_above):
    return jnp.where(
        row == TILE_ROWS - 1,
        NEAR * one_above - FAR * two_above,
        jnp.where(row == TILE_ROWS - 2, -FAR * one_above, 0.0),
    )


def times(left, right):
    return (
        left[0] * right[0] + left[1] * right[2],
        left[0] * right[1] + left[1] * right[3],
        left[2] * right[0] + left[3] * right[2],
        left[2] * right[1] + left[3] * right[3],
    )


def apply(matrix, vector):
    return (
        matrix[0] * vector[0] + matrix[1] * vector[1],
        matrix[2] * vector[0] + matrix[3] * vector[1],
    )


def plus(left, right):
    return tuple(a + b for a, b in zip(left, right))


def kernel(
    levs,
    tiles,
    adjoint_hbm,
    courant_hbm,
    metric_hbm,
    pivot_hbm,
    lower_hbm,
    upper_hbm,
    stepped,
    adjoint,
    courant,
    metric,
    pivot,
    lower,
    upper,
    forcing,
    narrow_gain,
    narrow_forcing,
    edge_send,
    edge_recv,
    side_send,
    side_recv,
    block_send,
    block_recv,
    carry_send,
    carry_recv,
    state_send,
    state_recv,
    edge_block_send,
    edge_block_recv,
    extra_send,
    extra_recv,
    tail_send,
    tail_recv,
    load_sem,
    edge_sems,
    side_sems,
    block_sems,
    carry_sems,
    state_sems,
    edge_block_sems,
    extra_sems,
    tail_sems,
    open_sem,
):
    lev = lax.axis_index("lev")
    tile = lax.axis_index("tile")
    levels, rows, lanes = adjoint.shape[1:]
    right = lax.rem(tile + 1, tiles)
    left = lax.rem(tile + tiles - 1, tiles)

    def peer(offset):
        return lax.rem(lev + offset, levs)

    def slot_of(source):
        return lax.rem(lev + levs - source, levs)

    parts = block_send.shape[0]
    first = (levs - parts) // 2

    def solves(device):
        return jnp.logical_and(device >= first, device < first + parts)

    solver = solves(lev)

    chief = 1

    opener = tile == 0
    answerer = tile == tiles - 1

    barrier = pltpu.get_barrier_semaphore()
    for target, is_long in ((left, opener), (right, answerer)):

        @pl.when(jnp.logical_not(is_long))
        def _():
            pl.semaphore_signal(barrier, inc=1, device_id=(lev, target), device_id_type=MESH)

    for offset in range(1, levs):
        pl.semaphore_signal(barrier, inc=1, device_id=(peer(offset), tile), device_id_type=MESH)

    halves = lanes // TILE_LANES
    bands = rows // TILE_ROWS

    order = (
        [(adjoint_hbm.at[field], adjoint.at[field]) for field in (0, 2, 4)]
        + [(courant_hbm.at[0], courant.at[0]), (metric_hbm.at[0], metric.at[0])]
        + [(lower_hbm, lower), (upper_hbm, upper)]
        + [(courant_hbm.at[1], courant.at[1]), (metric_hbm.at[1], metric.at[1])]
        + [(adjoint_hbm.at[field], adjoint.at[field]) for field in (1, 3)]
        + [(pivot_hbm, pivot)]
    )
    loads = [
        pltpu.make_async_copy(source, target, load_sem.at[i])
        for i, (source, target) in enumerate(order)
    ]
    for load in loads[:5]:
        load.start()
    for load in loads[:5]:
        load.wait()
    for load in loads[5:]:
        load.start()

    def weighted(level, field):
        along = courant[0, level] * adjoint[field, level]
        if field == 4:
            along = along + metric[0, level] * adjoint[0, level]
        return along

    def edges(level, carry):
        for place, field in ((0, 2), (1, 4)):
            along = weighted(level, field)
            ends = [along[i : i + 1] for i in (0, 1, rows - 2, rows - 1)]
            sent = (
                (-FAR * ends[0], NEAR * ends[0] - FAR * ends[1]),
                (FAR * ends[2] - NEAR * ends[3], FAR * ends[3]),
            )
            for direction in range(2):
                for half in range(halves):
                    for i in range(2):
                        edge_send[direction, place, level, 2 * half + i : 2 * half + i + 1] = sent[
                            direction
                        ][i][:, half * TILE_LANES : (half + 1) * TILE_LANES]
        return carry

    lax.fori_loop(0, levels, edges, 0, unroll=True)

    @pl.when(jnp.logical_not(opener))
    def _():
        pl.semaphore_wait(barrier, levs + 1)

    @pl.when(opener)
    def _():
        pl.semaphore_wait(barrier, levs)

    @pl.when(opener)
    def _():
        pl.semaphore_signal(barrier, inc=1, device_id=(lev, tiles - 1), device_id_type=MESH)

    @pl.when(answerer)
    def _():
        pl.semaphore_signal(open_sem, inc=1, device_id=(lev, 0), device_id_type=MESH)

    sides = (left, right)

    def to_side(source, target, sems, direction):
        return pltpu.make_async_remote_copy(
            src_ref=source.at[direction],
            dst_ref=target.at[direction],
            send_sem=sems.at[0, direction],
            recv_sem=sems.at[1, direction],
            device_id=(lev, sides[direction]),
            device_id_type=MESH,
        )

    def to_sides(source, target, sems):
        @pl.when(jnp.logical_not(opener))
        def _():
            to_side(source, target, sems, 0).start()

        to_side(source, target, sems, 1).start()
        return [to_side(source, target, sems, direction) for direction in range(2)]

    def level_copy(source, target, sems, offset, place):
        return pltpu.make_async_remote_copy(
            src_ref=source if place is None else source.at[place],
            dst_ref=target.at[offset],
            send_sem=sems.at[0, offset],
            recv_sem=sems.at[1, offset],
            device_id=(peer(offset), tile),
            device_id_type=MESH,
        )

    def part_of(device):
        return jnp.clip(device - first, 0, parts - 1)

    def to_solvers(source, target, sems, starting):
        for offset in range(1, levs):

            @pl.when(solves(peer(offset)))
            def _():
                copy = level_copy(source, target, sems, offset, part_of(peer(offset)))
                if starting:
                    copy.start()
                else:
                    copy.wait_send()

    def to_chief(source, target, sems, starting):
        for offset in range(1, levs):

            @pl.when(peer(offset) == chief)
            def _():
                copy = level_copy(source, target, sems, offset, None)
                if starting:
                    copy.start()
                else:
                    copy.wait_send()

    def at_chief(source, target, sems):
        target[0] = source[...]
        for offset in range(1, levs):
            level_copy(target.at[0], target, sems, offset, None).wait_recv()

    def at_solver(source, target, sems):
        target[0] = source[part_of(lev)]
        for offset in range(1, levs):
            level_copy(source, target, sems, offset, 0).wait_recv()

    edge_copies = to_sides(edge_send, edge_recv, edge_sems)

    for load in loads[5:7]:
        load.wait()

    tile_shape = (TILE_ROWS, TILE_LANES)
    row = lax.broadcasted_iota(jnp.int32, tile_shape, 0)

    def part(index):
        return pl.ds(pl.multiple_of(index * TILE_LANES, TILE_LANES), TILE_LANES)

    def summarise(index, carry):
        for band in range(bands):
            where = (pl.ds(band * TILE_ROWS, TILE_ROWS), part(index))

            def gain(ref, level):
                return tuple(ref[entry, level, where[0], where[1]] for entry in range(4))

            down = [gain(lower, 0)]
            for level in range(1, levels):
                down.append(times(gain(lower, level), down[-1]))
            up = gain(upper, levels - 1)
            mixed = down[-1]
            for level in range(levels - 2, -1, -1):
                step = gain(upper, level)
                mixed = plus(times(step, mixed), down[level])
                up = times(step, up)
            target = band * halves + index
            for place, matrix in enumerate((down[-1], up, mixed)):
                for entry in range(4):
                    block_send[target, 4 * place + entry] = matrix[entry]
        return carry

    lax.fori_loop(0, halves, summarise, 0)
    to_solvers(block_send, block_recv, block_sems, True)


    for load in loads[7:]:
        load.wait()

    def critical(level, carry):
        for field in (2, 4):
            here = adjoint[field, level]
            across = courant[1, level] * here
            if field == 4:
                across = across + metric[1, level] * adjoint[1, level]
            along = rows_inside(weighted(level, field))
            stepped[field, level] = here + along + lanes_around(across)
        return carry

    lax.fori_loop(0, levels, critical, 0)

    def force(index, carry):
        lane_part = part(index)
        for band in range(bands):
            row_part = pl.ds(band * TILE_ROWS, TILE_ROWS)

            def gain(ref, level):
                return tuple(ref[entry, level, row_part, lane_part] for entry in range(4))

            falling = []
            for level in range(levels):
                pair = tuple(stepped[field, level, row_part, lane_part] for field in (2, 4))
                fresh = apply(gain(pivot, level), pair)
                for place in range(2):
                    forcing[place, level, row_part, lane_part] = fresh[place]
                if falling:
                    fresh = plus(apply(gain(lower, level), falling[-1]), fresh)
                falling.append(fresh)
            rising = falling[-1]
            for level in range(levels - 2, -1, -1):
                rising = plus(apply(gain(upper, level), rising), falling[level])
            target = band * halves + index
            for place, value in enumerate(falling[-1] + rising):
                carry_send[target, place] = value
        return carry

    lax.fori_loop(0, halves, force, 0)
    to_solvers(carry_send, carry_recv, carry_sems, True)

    def passive(level, carry):
        drift = courant[0, level]
        side = courant[1, level]
        for place, field in enumerate((0, 1, 3)):
            here = adjoint[field, level]
            along = drift * here
            side_send[0, place, level] = along[:2]
            side_send[1, place, level] = along[rows - 2 :]
            stepped[field, level] = here + rows_inside(along) + lanes_around(side * here)
        return carry

    lax.fori_loop(0, levels, passive, 0)

    def turned(values, pairs):
        shift = 2 * (pairs % parts)
        return pltpu.roll(values, shift, 0) if shift else values

    def at_pair(pair):
        return jnp.logical_and(row >= 2 * pair, row < 2 * pair + 2)

    def home(index):
        return (parts - 1) * (index // halves)

    def ends_of(load):
        total = None
        for index in range(parts):
            band, half = divmod(index, halves)
            values = load(
                pl.ds(band * TILE_ROWS, TILE_ROWS), pl.ds(half * TILE_LANES, TILE_LANES)
            )
            values = turned(values, index - home(index))
            total = values if total is None else jnp.where(at_pair(index), values, total)
        return total

    def narrow(level, carry):
        for place, ref in enumerate((pivot, lower, upper)):
            for entry in range(4):
                narrow_gain[place, entry, level] = ends_of(
                    lambda row_part, lane_part: ref[entry, level, row_part, lane_part]
                )
        for place in range(2):
            narrow_forcing[place, level] = ends_of(
                lambda row_part, lane_part: forcing[place, level, row_part, lane_part]
            )
        return carry

    lax.fori_loop(0, levels, narrow, 0)

    for entry in range(12):
        total = None
        for index in range(parts):
            values = turned(block_send[index, entry], index - home(index))
            total = values if total is None else jnp.where(at_pair(index), values, total)
        edge_block_send[entry] = total
    to_chief(edge_block_send, edge_block_recv, edge_block_sems, True)
    side_copies = to_sides(side_send, side_recv, side_sems)

    def narrow_matrix(place, level):
        return tuple(narrow_gain[place, entry, level] for entry in range(4))

    def mend():
        for copy in edge_copies:
            copy.wait_recv()
        falling = []
        for level in range(levels):
            pair = tuple(
                jnp.concatenate([edge_recv[1, place, level], edge_recv[0, place, level]], axis=0)
                for place in range(2)
            )
            fresh = apply(narrow_matrix(0, level), pair)
            fresh = plus(tuple(narrow_forcing[place, level] for place in range(2)), fresh)
            for place in range(2):
                narrow_forcing[place, level] = fresh[place]
            if falling:
                fresh = plus(apply(narrow_matrix(1, level), falling[-1]), fresh)
            falling.append(fresh)
        rising = falling[-1]
        for level in range(levels - 2, -1, -1):
            rising = plus(apply(narrow_matrix(2, level), rising), falling[level])
        for place, value in enumerate(falling[-1] + rising):
            extra_send[place] = value
        to_chief(extra_send, extra_recv, extra_sems, True)

    pl.when(jnp.logical_not(opener))(mend)

    def solve(maps, vectors, target):
        def matrix(slot, place):
            return tuple(maps[slot, 4 * place + entry] for entry in range(4))

        def vector(slot, place):
            return tuple(vectors[slot, 2 * place + entry] for entry in range(2))

        nothing = jnp.zeros(tile_shape, jnp.float32)
        states = [(nothing, nothing)]
        for block in range(levs - 1):
            slot = slot_of(block)
            states.append(plus(apply(matrix(slot, 0), states[-1]), vector(slot, 0)))
        state = (nothing, nothing)
        for block in range(levs - 1, -1, -1):
            for entry, value in enumerate(states[block] + state):
                target[block, entry] = value
            if block:
                slot = slot_of(block)
                state = plus(
                    apply(matrix(slot, 1), state),
                    plus(apply(matrix(slot, 2), states[block]), vector(slot, 1)),
                )

    def send_back(source, target, sems):
        for offset in range(1, levs):
            level_copy(source, target, sems, offset, peer(offset)).start()
        target[0] = source[lev]

    @pl.when(solver)
    def _():
        at_solver(block_send, block_recv, block_sems)
        at_solver(carry_send, carry_recv, carry_sems)
        solve(block_recv, carry_recv, state_send)
        send_back(state_send, state_recv, state_sems)

    @pl.when(opener)
    def _():
        pl.semaphore_wait(open_sem, 1)
        to_side(edge_send, edge_recv, edge_sems, 0).start()
        to_side(side_send, side_recv, side_sems, 0).start()
        mend()

    @pl.when(lev == chief)
    def _():
        at_chief(edge_block_send, edge_block_recv, edge_block_sems)
        at_chief(extra_send, extra_recv, extra_sems)
        solve(edge_block_recv, extra_recv, tail_send)
        send_back(tail_send, tail_recv, tail_sems)

    for copy in side_copies:
        copy.wait_recv()

    def finish(level, carry):
        wide = lax.broadcasted_iota(jnp.int32, (TILE_ROWS, lanes), 0)
        for place, field in enumerate((0, 1, 3)):
            top = pl.ds(0, TILE_ROWS)
            bottom = pl.ds(rows - TILE_ROWS, TILE_ROWS)
            stepped[field, level, top] += low_edge(
                wide,
                side_recv[1, place, level, pl.ds(0, 1)],
                side_recv[1, place, level, pl.ds(1, 1)],
            )
            stepped[field, level, bottom] += high_edge(
                wide,
                side_recv[0, place, level, pl.ds(0, 1)],
                side_recv[0, place, level, pl.ds(1, 1)],
            )
        return carry

    lax.fori_loop(0, levels, finish, 0)

    for offset in range(1, levs):

        @pl.when(solves(lax.rem(lev + levs - offset, levs)))
        def _():
            level_copy(state_send, state_recv, state_sems, offset, 0).wait_recv()


    def settle(index, carry):
        lane_part = part(index)
        for band in range(bands):
            row_part = pl.ds(band * TILE_ROWS, TILE_ROWS)

            def gain(ref, level):
                return tuple(ref[entry, level, row_part, lane_part] for entry in range(4))

            slot = slot_of(first + band * halves + index)
            state = (state_recv[slot, 0], state_recv[slot, 1])
            falling = []
            for level in range(levels):
                fresh = tuple(forcing[place, level, row_part, lane_part] for place in range(2))
                state = plus(apply(gain(lower, level), state), fresh)
                falling.append(state)
            state = (state_recv[slot, 2], state_recv[slot, 3])
            for level in range(levels - 1, -1, -1):
                state = plus(apply(gain(upper, level), state), falling[level])
                stepped[2, level, row_part, lane_part] = state[0]
                stepped[4, level, row_part, lane_part] = state[1]
        return carry

    lax.fori_loop(0, halves, settle, 0)
    for offset in range(1, levs):

        @pl.when(lax.rem(lev + levs - offset, levs) == chief)
        def _():
            level_copy(tail_send, tail_recv, tail_sems, offset, 0).wait_recv()

    entering = [tail_recv[slot_of(chief), place] for place in range(4)]
    state = tuple(entering[:2])
    falling = []
    for level in range(levels):
        fresh = tuple(narrow_forcing[place, level] for place in range(2))
        state = plus(apply(narrow_matrix(1, level), state), fresh)
        falling.append(state)
    state = tuple(entering[2:])
    for level in range(levels - 1, -1, -1):
        state = plus(apply(narrow_matrix(2, level), state), falling[level])
        for place, field in ((0, 2), (1, 4)):
            for index in range(parts):
                band, half = divmod(index, halves)
                edge = band * (rows - 2)
                stepped[
                    field,
                    level,
                    edge : edge + 2,
                    half * TILE_LANES : (half + 1) * TILE_LANES,
                ] = state[place][2 * index : 2 * index + 2]
    for copy in edge_copies + side_copies:
        copy.wait_send()
    to_solvers(block_send, block_recv, block_sems, False)
    to_solvers(carry_send, carry_recv, carry_sems, False)
    to_chief(edge_block_send, edge_block_recv, edge_block_sems, False)
    to_chief(extra_send, extra_recv, extra_sems, False)

    @pl.when(solver)
    def _():
        for offset in range(1, levs):
            level_copy(state_send, state_recv, state_sems, offset, 0).wait_send()

    @pl.when(lev == chief)
    def _():
        for offset in range(1, levs):
            level_copy(tail_send, tail_recv, tail_sems, offset, 0).wait_send()


def local(levs, tiles, adjoint, courant, metric, pivot_inverse, lower_gain, upper_gain):
    fields, levels, rows, lanes = adjoint.shape
    arrays = (adjoint, courant, metric, pivot_inverse, lower_gain, upper_gain)
    small = (TILE_ROWS, TILE_LANES)
    parts = rows * lanes // (TILE_ROWS * TILE_LANES)

    def vmem(*shape):
        return pltpu.VMEM(shape, jnp.float32)

    return pl.pallas_call(
        functools.partial(kernel, levs, tiles),
        out_shape=pltpu.VMEM(adjoint.shape, jnp.float32),
        in_specs=[pl.BlockSpec(memory_space=pl.ANY)] * len(arrays),
        out_specs=pl.BlockSpec(memory_space=pltpu.VMEM),
        scratch_shapes=[vmem(*array.shape) for array in arrays]
        + [
            vmem(2, levels, rows, lanes),
            vmem(3, 4, levels, *small),
            vmem(2, levels, *small),
            vmem(2, 2, levels, parts, TILE_LANES),
            vmem(2, 2, levels, parts, TILE_LANES),
            vmem(2, 3, levels, 2, lanes),
            vmem(2, 3, levels, 2, lanes),
            vmem(parts, 12, *small),
            vmem(levs, 12, *small),
            vmem(parts, 4, *small),
            vmem(levs, 4, *small),
            vmem(levs, 4, *small),
            vmem(levs, 4, *small),
            vmem(12, *small),
            vmem(levs, 12, *small),
            vmem(4, *small),
            vmem(levs, 4, *small),
            vmem(levs, 4, *small),
            vmem(levs, 4, *small),
            pltpu.SemaphoreType.DMA((12,)),
            pltpu.SemaphoreType.DMA((2, 2)),
            pltpu.SemaphoreType.DMA((2, 2)),
            pltpu.SemaphoreType.DMA((2, levs)),
            pltpu.SemaphoreType.DMA((2, levs)),
            pltpu.SemaphoreType.DMA((2, levs)),
            pltpu.SemaphoreType.DMA((2, levs)),
            pltpu.SemaphoreType.DMA((2, levs)),
            pltpu.SemaphoreType.DMA((2, levs)),
            pltpu.SemaphoreType.REGULAR,
        ],
        compiler_params=pltpu.CompilerParams(collective_id=0, has_side_effects=True),
    )(*arrays)


def solution(mesh):
    placed = P(None, "lev", "tile", None)
    return jax.shard_map(
        functools.partial(local, mesh.shape["lev"], mesh.shape["tile"]),
        mesh=mesh,
        in_specs=(placed,) * 6,
        out_specs=placed,
        check_vma=False,
    )
```

```python
import functools

import jax
import jax.numpy as jnp
from jax import lax
from jax.experimental import pallas as pl
from jax.experimental.pallas import tpu as pltpu
from jax.sharding import PartitionSpec as P

MESH = pl.DeviceIdType.MESH
NEAR = 8.0 / 12.0
FAR = 1.0 / 12.0
TILE_ROWS = 8
TILE_LANES = 128


def difference(ahead_one, behind_one, ahead_two, behind_two):
    return NEAR * (ahead_one - behind_one) - FAR * (ahead_two - behind_two)


def rows_inside(values):
    count = values.shape[0]
    row = lax.broadcasted_iota(jnp.int32, values.shape, 0)
    return difference(
        jnp.where(row < count - 1, pltpu.roll(values, count - 1, 0), 0.0),
        jnp.where(row >= 1, pltpu.roll(values, 1, 0), 0.0),
        jnp.where(row < count - 2, pltpu.roll(values, count - 2, 0), 0.0),
        jnp.where(row >= 2, pltpu.roll(values, 2, 0), 0.0),
    )


def lanes_around(values):
    count = values.shape[1]
    return difference(
        pltpu.roll(values, count - 1, 1),
        pltpu.roll(values, 1, 1),
        pltpu.roll(values, count - 2, 1),
        pltpu.roll(values, 2, 1),
    )


def low_edge(row, two_below, one_below):
    return jnp.where(
        row == 0, FAR * two_below - NEAR * one_below, jnp.where(row == 1, FAR * one_below, 0.0)
    )


def high_edge(row, one_above, two_above):
    return jnp.where(
        row == TILE_ROWS - 1,
        NEAR * one_above - FAR * two_above,
        jnp.where(row == TILE_ROWS - 2, -FAR * one_above, 0.0),
    )


def times(left, right):
    return (
        left[0] * right[0] + left[1] * right[2],
        left[0] * right[1] + left[1] * right[3],
        left[2] * right[0] + left[3] * right[2],
        left[2] * right[1] + left[3] * right[3],
    )


def apply(matrix, vector):
    return (
        matrix[0] * vector[0] + matrix[1] * vector[1],
        matrix[2] * vector[0] + matrix[3] * vector[1],
    )


def plus(left, right):
    return tuple(a + b for a, b in zip(left, right))


def kernel(
    levs,
    tiles,
    adjoint_hbm,
    courant_hbm,
    metric_hbm,
    pivot_hbm,
    lower_hbm,
    upper_hbm,
    stepped,
    adjoint,
    courant,
    metric,
    pivot,
    lower,
    upper,
    forcing,
    narrow_gain,
    narrow_forcing,
    edge_send,
    edge_recv,
    side_send,
    side_recv,
    block_send,
    block_recv,
    carry_send,
    carry_recv,
    state_send,
    state_recv,
    edge_block_send,
    edge_block_recv,
    extra_send,
    extra_recv,
    tail_send,
    tail_recv,
    load_sem,
    edge_sems,
    side_sems,
    block_sems,
    carry_sems,
    state_sems,
    edge_block_sems,
    extra_sems,
    tail_sems,
    open_sem,
):
    lev = lax.axis_index("lev")
    tile = lax.axis_index("tile")
    levels, rows, lanes = adjoint.shape[1:]
    right = lax.rem(tile + 1, tiles)
    left = lax.rem(tile + tiles - 1, tiles)

    def peer(offset):
        return lax.rem(lev + offset, levs)

    def slot_of(source):
        return lax.rem(lev + levs - source, levs)

    parts = block_send.shape[0]
    first = (levs - parts) // 2

    def solves(device):
        return jnp.logical_and(device >= first, device < first + parts)

    solver = solves(lev)

    chief = 1

    opener = tile == 0
    answerer = tile == tiles - 1

    barrier = pltpu.get_barrier_semaphore()
    for target, is_long in ((left, opener), (right, answerer)):

        @pl.when(jnp.logical_not(is_long))
        def _():
            pl.semaphore_signal(barrier, inc=1, device_id=(lev, target), device_id_type=MESH)

    for offset in range(1, levs):
        pl.semaphore_signal(barrier, inc=1, device_id=(peer(offset), tile), device_id_type=MESH)

    halves = lanes // TILE_LANES
    bands = rows // TILE_ROWS

    order = (
        [(adjoint_hbm.at[field], adjoint.at[field]) for field in (0, 2, 4)]
        + [(courant_hbm.at[0], courant.at[0]), (metric_hbm.at[0], metric.at[0])]
        + [(lower_hbm, lower), (upper_hbm, upper)]
        + [(courant_hbm.at[1], courant.at[1]), (metric_hbm.at[1], metric.at[1])]
        + [(adjoint_hbm.at[field], adjoint.at[field]) for field in (1, 3)]
        + [(pivot_hbm, pivot)]
    )
    loads = [
        pltpu.make_async_copy(source, target, load_sem.at[i])
        for i, (source, target) in enumerate(order)
    ]
    for load in loads[:5]:
        load.start()
    for load in loads[:5]:
        load.wait()
    for load in loads[5:]:
        load.start()

    def weighted(level, field):
        along = courant[0, level] * adjoint[field, level]
        if field == 4:
            along = along + metric[0, level] * adjoint[0, level]
        return along

    def edges(level, carry):
        for place, field in ((0, 2), (1, 4)):
            along = weighted(level, field)
            ends = [along[i : i + 1] for i in (0, 1, rows - 2, rows - 1)]
            sent = (
                (-FAR * ends[0], NEAR * ends[0] - FAR * ends[1]),
                (FAR * ends[2] - NEAR * ends[3], FAR * ends[3]),
            )
            for direction in range(2):
                for half in range(halves):
                    for i in range(2):
                        edge_send[direction, place, level, 2 * half + i : 2 * half + i + 1] = sent[
                            direction
                        ][i][:, half * TILE_LANES : (half + 1) * TILE_LANES]
        return carry

    lax.fori_loop(0, levels, edges, 0, unroll=True)

    @pl.when(jnp.logical_not(opener))
    def _():
        pl.semaphore_wait(barrier, levs + 1)

    @pl.when(opener)
    def _():
        pl.semaphore_wait(barrier, levs)

    @pl.when(opener)
    def _():
        pl.semaphore_signal(barrier, inc=1, device_id=(lev, tiles - 1), device_id_type=MESH)

    @pl.when(answerer)
    def _():
        pl.semaphore_signal(open_sem, inc=1, device_id=(lev, 0), device_id_type=MESH)

    sides = (left, right)

    def to_side(source, target, sems, direction):
        return pltpu.make_async_remote_copy(
            src_ref=source.at[direction],
            dst_ref=target.at[direction],
            send_sem=sems.at[0, direction],
            recv_sem=sems.at[1, direction],
            device_id=(lev, sides[direction]),
            device_id_type=MESH,
        )

    def to_sides(source, target, sems):
        @pl.when(jnp.logical_not(opener))
        def _():
            to_side(source, target, sems, 0).start()

        to_side(source, target, sems, 1).start()
        return [to_side(source, target, sems, direction) for direction in range(2)]

    def level_copy(source, target, sems, offset, place):
        return pltpu.make_async_remote_copy(
            src_ref=source if place is None else source.at[place],
            dst_ref=target.at[offset],
            send_sem=sems.at[0, offset],
            recv_sem=sems.at[1, offset],
            device_id=(peer(offset), tile),
            device_id_type=MESH,
        )

    def part_of(device):
        return jnp.clip(device - first, 0, parts - 1)

    def to_solvers(source, target, sems, starting):
        for offset in range(1, levs):

            @pl.when(solves(peer(offset)))
            def _():
                copy = level_copy(source, target, sems, offset, part_of(peer(offset)))
                if starting:
                    copy.start()
                else:
                    copy.wait_send()

    def to_chief(source, target, sems, starting):
        for offset in range(1, levs):

            @pl.when(peer(offset) == chief)
            def _():
                copy = level_copy(source, target, sems, offset, None)
                if starting:
                    copy.start()
                else:
                    copy.wait_send()

    def at_chief(source, target, sems):
        target[0] = source[...]
        for offset in range(1, levs):
            level_copy(target.at[0], target, sems, offset, None).wait_recv()

    def at_solver(source, target, sems):
        target[0] = source[part_of(lev)]
        for offset in range(1, levs):
            level_copy(source, target, sems, offset, 0).wait_recv()

    edge_copies = to_sides(edge_send, edge_recv, edge_sems)

    for load in loads[5:7]:
        load.wait()

    tile_shape = (TILE_ROWS, TILE_LANES)
    row = lax.broadcasted_iota(jnp.int32, tile_shape, 0)

    def part(index):
        return pl.ds(pl.multiple_of(index * TILE_LANES, TILE_LANES), TILE_LANES)

    def summarise(index, carry):
        for band in range(bands):
            where = (pl.ds(band * TILE_ROWS, TILE_ROWS), part(index))

            def gain(ref, level):
                return tuple(ref[entry, level, where[0], where[1]] for entry in range(4))

            down = [gain(lower, 0)]
            for level in range(1, levels):
                down.append(times(gain(lower, level), down[-1]))
            up = gain(upper, levels - 1)
            mixed = down[-1]
            for level in range(levels - 2, -1, -1):
                step = gain(upper, level)
                mixed = plus(times(step, mixed), down[level])
                up = times(step, up)
            target = band * halves + index
            for place, matrix in enumerate((down[-1], up, mixed)):
                for entry in range(4):
                    block_send[target, 4 * place + entry] = matrix[entry]
        return carry

    lax.fori_loop(0, halves, summarise, 0)
    to_solvers(block_send, block_recv, block_sems, True)


    for load in loads[7:]:
        load.wait()

    def critical(level, carry):
        for field in (2, 4):
            here = adjoint[field, level]
            across = courant[1, level] * here
            if field == 4:
                across = across + metric[1, level] * adjoint[1, level]
            along = rows_inside(weighted(level, field))
            stepped[field, level] = here + along + lanes_around(across)
        return carry

    lax.fori_loop(0, levels, critical, 0)

    def force(index, carry):
        lane_part = part(index)
        for band in range(bands):
            row_part = pl.ds(band * TILE_ROWS, TILE_ROWS)

            def gain(ref, level):
                return tuple(ref[entry, level, row_part, lane_part] for entry in range(4))

            falling = []
            for level in range(levels):
                pair = tuple(stepped[field, level, row_part, lane_part] for field in (2, 4))
                fresh = apply(gain(pivot, level), pair)
                for place in range(2):
                    forcing[place, level, row_part, lane_part] = fresh[place]
                if falling:
                    fresh = plus(apply(gain(lower, level), falling[-1]), fresh)
                falling.append(fresh)
            rising = falling[-1]
            for level in range(levels - 2, -1, -1):
                rising = plus(apply(gain(upper, level), rising), falling[level])
            target = band * halves + index
            for place, value in enumerate(falling[-1] + rising):
                carry_send[target, place] = value
        return carry

    lax.fori_loop(0, halves, force, 0)
    to_solvers(carry_send, carry_recv, carry_sems, True)

    def passive(level, carry):
        drift = courant[0, level]
        side = courant[1, level]
        for place, field in enumerate((0, 1, 3)):
            here = adjoint[field, level]
            along = drift * here
            side_send[0, place, level] = along[:2]
            side_send[1, place, level] = along[rows - 2 :]
            stepped[field, level] = here + rows_inside(along) + lanes_around(side * here)
        return carry

    lax.fori_loop(0, levels, passive, 0)

    def turned(values, pairs):
        shift = 2 * (pairs % parts)
        return pltpu.roll(values, shift, 0) if shift else values

    def at_pair(pair):
        return jnp.logical_and(row >= 2 * pair, row < 2 * pair + 2)

    def home(index):
        return (parts - 1) * (index // halves)

    def ends_of(load):
        total = None
        for index in range(parts):
            band, half = divmod(index, halves)
            values = load(
                pl.ds(band * TILE_ROWS, TILE_ROWS), pl.ds(half * TILE_LANES, TILE_LANES)
            )
            values = turned(values, index - home(index))
            total = values if total is None else jnp.where(at_pair(index), values, total)
        return total

    def narrow(level, carry):
        for place, ref in enumerate((pivot, lower, upper)):
            for entry in range(4):
                narrow_gain[place, entry, level] = ends_of(
                    lambda row_part, lane_part: ref[entry, level, row_part, lane_part]
                )
        for place in range(2):
            narrow_forcing[place, level] = ends_of(
                lambda row_part, lane_part: forcing[place, level, row_part, lane_part]
            )
        return carry

    lax.fori_loop(0, levels, narrow, 0)

    for entry in range(12):
        total = None
        for index in range(parts):
            values = turned(block_send[index, entry], index - home(index))
            total = values if total is None else jnp.where(at_pair(index), values, total)
        edge_block_send[entry] = total
    to_chief(edge_block_send, edge_block_recv, edge_block_sems, True)
    side_copies = to_sides(side_send, side_recv, side_sems)

    def narrow_matrix(place, level):
        return tuple(narrow_gain[place, entry, level] for entry in range(4))

    def mend():
        for copy in edge_copies:
            copy.wait_recv()
        falling = []
        for level in range(levels):
            pair = tuple(
                jnp.concatenate([edge_recv[1, place, level], edge_recv[0, place, level]], axis=0)
                for place in range(2)
            )
            fresh = apply(narrow_matrix(0, level), pair)
            fresh = plus(tuple(narrow_forcing[place, level] for place in range(2)), fresh)
            for place in range(2):
                narrow_forcing[place, level] = fresh[place]
            if falling:
                fresh = plus(apply(narrow_matrix(1, level), falling[-1]), fresh)
            falling.append(fresh)
        rising = falling[-1]
        for level in range(levels - 2, -1, -1):
            rising = plus(apply(narrow_matrix(2, level), rising), falling[level])
        for place, value in enumerate(falling[-1] + rising):
            extra_send[place] = value
        to_chief(extra_send, extra_recv, extra_sems, True)

    pl.when(jnp.logical_not(opener))(mend)

    def solve(maps, vectors, target):
        def matrix(slot, place):
            return tuple(maps[slot, 4 * place + entry] for entry in range(4))

        def vector(slot, place):
            return tuple(vectors[slot, 2 * place + entry] for entry in range(2))

        nothing = jnp.zeros(tile_shape, jnp.float32)
        states = [(nothing, nothing)]
        for block in range(levs - 1):
            slot = slot_of(block)
            states.append(plus(apply(matrix(slot, 0), states[-1]), vector(slot, 0)))
        state = (nothing, nothing)
        for block in range(levs - 1, -1, -1):
            for entry, value in enumerate(states[block] + state):
                target[block, entry] = value
            if block:
                slot = slot_of(block)
                state = plus(
                    apply(matrix(slot, 1), state),
                    plus(apply(matrix(slot, 2), states[block]), vector(slot, 1)),
                )

    def send_back(source, target, sems):
        for offset in range(1, levs):
            level_copy(source, target, sems, offset, peer(offset)).start()
        target[0] = source[lev]

    @pl.when(solver)
    def _():
        at_solver(block_send, block_recv, block_sems)
        at_solver(carry_send, carry_recv, carry_sems)
        solve(block_recv, carry_recv, state_send)
        send_back(state_send, state_recv, state_sems)

    @pl.when(opener)
    def _():
        pl.semaphore_wait(open_sem, 1)
        to_side(edge_send, edge_recv, edge_sems, 0).start()
        to_side(side_send, side_recv, side_sems, 0).start()
        mend()

    for offset in range(1, levs):

        @pl.when(solves(lax.rem(lev + levs - offset, levs)))
        def _():
            level_copy(state_send, state_recv, state_sems, offset, 0).wait_recv()


    def settle(index, carry):
        lane_part = part(index)
        for band in range(bands):
            row_part = pl.ds(band * TILE_ROWS, TILE_ROWS)

            def gain(ref, level):
                return tuple(ref[entry, level, row_part, lane_part] for entry in range(4))

            slot = slot_of(first + band * halves + index)
            state = (state_recv[slot, 0], state_recv[slot, 1])
            falling = []
            for level in range(levels):
                fresh = tuple(forcing[place, level, row_part, lane_part] for place in range(2))
                state = plus(apply(gain(lower, level), state), fresh)
                falling.append(state)
            state = (state_recv[slot, 2], state_recv[slot, 3])
            for level in range(levels - 1, -1, -1):
                state = plus(apply(gain(upper, level), state), falling[level])
                stepped[2, level, row_part, lane_part] = state[0]
                stepped[4, level, row_part, lane_part] = state[1]
        return carry

    lax.fori_loop(0, halves, settle, 0)

    @pl.when(lev == chief)
    def _():
        at_chief(edge_block_send, edge_block_recv, edge_block_sems)
        at_chief(extra_send, extra_recv, extra_sems)
        solve(edge_block_recv, extra_recv, tail_send)
        send_back(tail_send, tail_recv, tail_sems)

    for copy in side_copies:
        copy.wait_recv()

    def finish(level, carry):
        wide = lax.broadcasted_iota(jnp.int32, (TILE_ROWS, lanes), 0)
        for place, field in enumerate((0, 1, 3)):
            top = pl.ds(0, TILE_ROWS)
            bottom = pl.ds(rows - TILE_ROWS, TILE_ROWS)
            stepped[field, level, top] += low_edge(
                wide,
                side_recv[1, place, level, pl.ds(0, 1)],
                side_recv[1, place, level, pl.ds(1, 1)],
            )
            stepped[field, level, bottom] += high_edge(
                wide,
                side_recv[0, place, level, pl.ds(0, 1)],
                side_recv[0, place, level, pl.ds(1, 1)],
            )
        return carry

    lax.fori_loop(0, levels, finish, 0)

    for offset in range(1, levs):

        @pl.when(lax.rem(lev + levs - offset, levs) == chief)
        def _():
            level_copy(tail_send, tail_recv, tail_sems, offset, 0).wait_recv()

    entering = [tail_recv[slot_of(chief), place] for place in range(4)]
    state = tuple(entering[:2])
    falling = []
    for level in range(levels):
        fresh = tuple(narrow_forcing[place, level] for place in range(2))
        state = plus(apply(narrow_matrix(1, level), state), fresh)
        falling.append(state)
    state = tuple(entering[2:])
    for level in range(levels - 1, -1, -1):
        state = plus(apply(narrow_matrix(2, level), state), falling[level])
        for place, field in ((0, 2), (1, 4)):
            for index in range(parts):
                band, half = divmod(index, halves)
                edge = band * (rows - 2)
                stepped[
                    field,
                    level,
                    edge : edge + 2,
                    half * TILE_LANES : (half + 1) * TILE_LANES,
                ] = state[place][2 * index : 2 * index + 2]
    for copy in edge_copies + side_copies:
        copy.wait_send()
    to_solvers(block_send, block_recv, block_sems, False)
    to_solvers(carry_send, carry_recv, carry_sems, False)
    to_chief(edge_block_send, edge_block_recv, edge_block_sems, False)
    to_chief(extra_send, extra_recv, extra_sems, False)

    @pl.when(solver)
    def _():
        for offset in range(1, levs):
            level_copy(state_send, state_recv, state_sems, offset, 0).wait_send()

    @pl.when(lev == chief)
    def _():
        for offset in range(1, levs):
            level_copy(tail_send, tail_recv, tail_sems, offset, 0).wait_send()


def local(levs, tiles, adjoint, courant, metric, pivot_inverse, lower_gain, upper_gain):
    fields, levels, rows, lanes = adjoint.shape
    arrays = (adjoint, courant, metric, pivot_inverse, lower_gain, upper_gain)
    small = (TILE_ROWS, TILE_LANES)
    parts = rows * lanes // (TILE_ROWS * TILE_LANES)

    def vmem(*shape):
        return pltpu.VMEM(shape, jnp.float32)

    return pl.pallas_call(
        functools.partial(kernel, levs, tiles),
        out_shape=pltpu.VMEM(adjoint.shape, jnp.float32),
        in_specs=[pl.BlockSpec(memory_space=pl.ANY)] * len(arrays),
        out_specs=pl.BlockSpec(memory_space=pltpu.VMEM),
        scratch_shapes=[vmem(*array.shape) for array in arrays]
        + [
            vmem(2, levels, rows, lanes),
            vmem(3, 4, levels, *small),
            vmem(2, levels, *small),
            vmem(2, 2, levels, parts, TILE_LANES),
            vmem(2, 2, levels, parts, TILE_LANES),
            vmem(2, 3, levels, 2, lanes),
            vmem(2, 3, levels, 2, lanes),
            vmem(parts, 12, *small),
            vmem(levs, 12, *small),
            vmem(parts, 4, *small),
            vmem(levs, 4, *small),
            vmem(levs, 4, *small),
            vmem(levs, 4, *small),
            vmem(12, *small),
            vmem(levs, 12, *small),
            vmem(4, *small),
            vmem(levs, 4, *small),
            vmem(levs, 4, *small),
            vmem(levs, 4, *small),
            pltpu.SemaphoreType.DMA((12,)),
            pltpu.SemaphoreType.DMA((2, 2)),
            pltpu.SemaphoreType.DMA((2, 2)),
            pltpu.SemaphoreType.DMA((2, levs)),
            pltpu.SemaphoreType.DMA((2, levs)),
            pltpu.SemaphoreType.DMA((2, levs)),
            pltpu.SemaphoreType.DMA((2, levs)),
            pltpu.SemaphoreType.DMA((2, levs)),
            pltpu.SemaphoreType.DMA((2, levs)),
            pltpu.SemaphoreType.REGULAR,
        ],
        compiler_params=pltpu.CompilerParams(collective_id=0, has_side_effects=True),
    )(*arrays)


def solution(mesh):
    placed = P(None, "lev", "tile", None)
    return jax.shard_map(
        functools.partial(local, mesh.shape["lev"], mesh.shape["tile"]),
        mesh=mesh,
        in_specs=(placed,) * 6,
        out_specs=placed,
        check_vma=False,
    )
```
